512 devices in a mesh: ta: 16 (over z), gz: 4 (over x), gy: 8 (over y, core).
Axes of the slice: x: 4, y: 4, z: 16, core: 2. Of those that a mesh axis runs over, the one named last changes fastest.
Arguments:
- state: float32 [16, 8, 16, 64, 128], P('ta', None, 'gz', 'gy'), may hold values from -6 to 6
- step_index: int32 [16], P('ta'), may hold values from 0 to 999
- sched_index: int32 [16], P('ta'), may hold values from 0 to 999
- coef_table: float32 [1000, 2], replicated, may hold values from 0.1 to 0.6
- time_weight: float32 [64, 64], replicated, may hold values from -0.75 to 0.75
- w_in: bfloat16 [3, 3, 3, 8, 64], replicated, may hold values from -0.4375 to 0.4375
- w_mid1: bfloat16 [3, 3, 3, 64, 64], replicated, may hold values from -0.15625 to 0.15625
- w_mid2: bfloat16 [3, 3, 3, 64, 64], replicated, may hold values from -0.15625 to 0.15625
- w_out: bfloat16 [3, 3, 3, 64, 8], replicated, may hold values from -0.15625 to 0.15625
Outputs:
- new_state: float32 [16, 8, 16, 64, 128], P('ta', None, 'gz', 'gy')
The draws below stay inside these ranges and needn't reach their ends.
All inputs are finite; a program needn't handle non-finite values.
Results may differ from the reference program's by a relative error of at most 0.0013.
Values may be sent and summed in bfloat16 or wider, within the bound.
No kernel may reach another device: no remote copies, remote signals or barrier semaphores. Data moves between devices by JAX's collectives and lax.ppermute only.
A program may use at most 64 MiB of HBM per device.

```python
import jax
import jax.numpy as jnp
from jax import lax

C = 8
HID = 64
TABLE = 1000
CX = 128
TSTEPS = 16
NZ = 16
NY = 64


def set_ends(array, stream_key, smallest, high):
    longest = array.shape.index(max(array.shape))
    spots = []
    for shift in (0, 1):
        where = [jax.random.randint(jax.random.fold_in(stream_key, axis), (), 0, length) for axis, length in enumerate(array.shape)]
        where[longest] = (where[longest] + shift) % array.shape[longest]
        spots.append(tuple(where))
    return array.at[spots[0]].set(smallest).at[spots[1]].set(high)


def level_of(own_key, extent, shards, least, largest):
    gain, own = 1.0, jax.random.fold_in(own_key, 6)
    for axis_at, shards_of in shards:
        draws = jnp.exp(jax.random.uniform(jax.random.fold_in(own, axis_at), (shards_of,), jnp.float32, least / len(shards), largest / len(shards)))
        gain = gain * jnp.repeat(draws, extent[axis_at] // shards_of).reshape([-1 if axis == axis_at else 1 for axis in range(len(extent))])
    return gain


def scatter_about(stream_key, extent, deviation, most, pieces=(), kind=jnp.bfloat16):
    array = deviation * jax.random.normal(stream_key, extent, jnp.float32)
    if pieces:
        array = array * level_of(stream_key, extent, pieces, -0.22, 0.18)
    return jnp.clip(array, -most, most).astype(kind)


def setup_inputs(seed: int = 0) -> dict:
    streams_of = jax.random.split(jax.random.key(seed), 10)
    state = scatter_about(streams_of[0], (TSTEPS, C, NZ, NY, CX), 1.0, 6.0, ((0, 16), (2, 4), (3, 8)), jnp.float32)
    step_index = set_ends(jax.random.randint(streams_of[1], (TSTEPS,), 0, TABLE), jax.random.fold_in(streams_of[1], 1), 0, TABLE - 1).astype(jnp.int32)
    sched_index = set_ends(jax.random.randint(streams_of[2], (TSTEPS,), 0, TABLE), jax.random.fold_in(streams_of[2], 1), 0, TABLE - 1).astype(jnp.int32)
    coef_table = jnp.clip(jax.random.uniform(streams_of[3], (TABLE, 2), jnp.float32, 0.1, 0.6), 0.1, 0.6)
    time_weight = scatter_about(streams_of[4], (HID, HID), HID ** -0.5, 0.75, (), jnp.float32)
    w_in = scatter_about(streams_of[5], (3, 3, 3, C, HID), (27 * C) ** -0.5, 0.4375)
    w_mid1 = scatter_about(streams_of[6], (3, 3, 3, HID, HID), (27 * HID) ** -0.5, 0.15625)
    w_mid2 = scatter_about(streams_of[7], (3, 3, 3, HID, HID), (27 * HID) ** -0.5, 0.15625)
    w_out = scatter_about(streams_of[8], (3, 3, 3, HID, C), (27 * HID) ** -0.5, 0.15625)
    return {"state": state, "step_index": step_index, "sched_index": sched_index, "coef_table": coef_table, "time_weight": time_weight, "w_in": w_in, "w_mid1": w_mid1, "w_mid2": w_mid2, "w_out": w_out}


def conv_same(volume, kernel):
    lhs = volume[None].astype(jnp.float32)
    rhs = jnp.transpose(kernel, (4, 3, 0, 1, 2)).astype(jnp.float32)
    result = lax.conv_general_dilated(lhs, rhs, (1, 1, 1), [(1, 1), (1, 1), (1, 1)], dimension_numbers=("NCDHW", "OIDHW", "NCDHW"), precision=lax.Precision.HIGHEST)
    return result[0]


def time_features(step, time_weight):
    half = HID // 2
    freqs = jnp.exp(-jnp.log(1000.0) * jnp.arange(half, dtype=jnp.float32) / half)
    angles = step.astype(jnp.float32) * freqs
    feats = jnp.concatenate([jnp.sin(angles), jnp.cos(angles)])
    return jnp.dot(feats, time_weight, precision=lax.Precision.HIGHEST)


def reference(state, step_index, sched_index, coef_table, time_weight, w_in, w_mid1, w_mid2, w_out):
    def one_slot(items):
        volume, step, sched = items
        inputs = volume.astype(jnp.bfloat16)
        bias = time_features(step, time_weight)
        hidden = jax.nn.silu(conv_same(inputs, w_in) + bias[:, None, None, None]).astype(jnp.bfloat16)
        hidden = jax.nn.silu(conv_same(hidden, w_mid1)).astype(jnp.bfloat16)
        hidden = jax.nn.silu(conv_same(hidden, w_mid2)).astype(jnp.bfloat16)
        network = conv_same(hidden, w_out)
        coef_a = coef_table[sched, 0]
        coef_b = coef_table[sched, 1]
        return coef_b * network - coef_a * volume

    drifts = lax.map(one_slot, (state, step_index, sched_index))
    summed = jnp.cumsum(drifts, axis=0)
    return state[0][None] + summed
```

```python
import functools

import jax
import jax.numpy as jnp
from jax import lax
from jax.experimental import pallas as pl
from jax.experimental.pallas import tpu as pltpu
from jax.sharding import PartitionSpec as P

F32 = jnp.float32
BF16 = jnp.bfloat16
DEPTH = 4


def banded(kernel, order):
    taps = jnp.transpose(kernel, (4, 1, 2, 0, 3))
    none = ((0, 0),) * 3
    first = jnp.pad(taps, none + ((0, 1), (0, 0)))
    second = jnp.pad(taps, none + ((1, 0), (0, 0)))
    return jnp.transpose(jnp.stack([first, second]), order)


def silu(x):
    return x / (1.0 + jnp.exp(-x))


def shifted(h):
    zero = jnp.zeros((h.shape[0], 1), h.dtype)
    left = jnp.concatenate([zero, h[:, :-1]], axis=1)
    right = jnp.concatenate([h[:, 1:], zero], axis=1)
    return left, h, right


def net_kernel(place, coef, x_ref, own_ref, bias_ref, w1_ref, w2_ref, w3_ref, w4_ref, out_ref, xs, h1, h2, h3):
    channels, nz, ny, nx = own_ref.shape
    hid = bias_ref.shape[0]
    z0, y0, z_size, y_size = place[0], place[1], place[2], place[3]

    def spread(rows, y):
        for d, v in enumerate(shifted(x_ref[y, rows, :])):
            xs[d, y, rows, :] = v

    for y in range(ny + 2 * DEPTH):
        spread(slice(None), y)

    def layer(src, w_ref, dst, depth, unit, dxs):
        off = DEPTH - depth
        pairs_z = (nz + 2 * off) // 2
        n_y = ny + 2 * off
        window = 4 * unit

        def step(zp, _):
            base = pl.multiple_of(zp * (2 * unit), 2 * unit)
            for y in range(0, n_y, 2):
                if depth == 1:
                    rhs = jnp.concatenate(
                        [
                            jnp.concatenate(
                                [src[dx, yy + dy, pl.ds(base, window), :] for dy in range(3) for dx in range(3)],
                                axis=0,
                            )
                            for yy in (y, y + 1)
                        ],
                        axis=1,
                    )
                    acc = jnp.dot(w_ref[...], rhs, preferred_element_type=F32)
                    acc = acc + jnp.tile(bias_ref[...], (2, 2))
                else:
                    acc = None
                    for k in range(9):
                        dy, dx = k // 3, k % 3
                        rhs = jnp.concatenate(
                            [src[dx, yy + dy, pl.ds(base, window), :] for yy in (y, y + 1)], axis=1
                        )
                        part = jnp.dot(
                            w_ref[:, k * window : (k + 1) * window], rhs, preferred_element_type=F32
                        )
                        acc = part if acc is None else acc + part
                h = silu(acc)
                for i in range(2):
                    gy = y0 - off + y + i
                    y_ok = jnp.logical_and(gy >= 0, gy < y_size)
                    for j in range(2):
                        gz = z0 - off + 2 * zp + j
                        ok = jnp.logical_and(y_ok, jnp.logical_and(gz >= 0, gz < z_size))
                        part = h[j * hid : (j + 1) * hid, i * nx : (i + 1) * nx]
                        part = jnp.where(ok, part, 0.0).astype(BF16)
                        rows = pl.ds(pl.multiple_of((2 * zp + j) * hid, hid), hid)
                        if dxs:
                            for d, v in enumerate(shifted(part)):
                                dst[d, y + i, rows, :] = v
                        else:
                            dst[y + i, rows, :] = part
            return 0

        lax.fori_loop(0, pairs_z, step, 0)

    layer(xs, w1_ref, h1, 1, channels, True)
    layer(h1, w2_ref, h2, 2, hid, True)
    layer(h2, w3_ref, h3, 3, hid, False)

    rows = 2 * channels
    lane = lax.broadcasted_iota(jnp.int32, (rows, nx), 1)
    a, b, first = coef[0], coef[1], coef[2]
    for zp in range(nz // 2):
        parts = []
        for y in range(0, ny + 2, 2):
            rhs = jnp.concatenate(
                [h3[yy, pl.ds(2 * zp * hid, 4 * hid), :] for yy in (y, y + 1)], axis=1
            )
            p = jnp.dot(w4_ref[...], rhs, preferred_element_type=F32)
            parts += [p[:, :nx], p[:, nx:]]
        nets = []
        for y in range(ny):
            t = [
                sum(parts[y + dy][(3 * dy + dx) * rows : (3 * dy + dx + 1) * rows] for dy in range(3))
                for dx in range(3)
            ]
            left = jnp.where(lane == 0, 0.0, pltpu.roll(t[0], 1, 1))
            right = jnp.where(lane == nx - 1, 0.0, pltpu.roll(t[2], nx - 1, 1))
            nets.append(left + t[1] + right)
        for j in range(2):
            net = jnp.stack([n[j * channels : (j + 1) * channels] for n in nets])
            net = jnp.transpose(net, (1, 0, 2))
            own = own_ref[:, 2 * zp + j]
            out_ref[:, 2 * zp + j] = b * net - a * own + first * own


def scan_kernel(d_ref, o_ref):
    total = d_ref[0]
    o_ref[0] = total
    for t in range(1, d_ref.shape[0]):
        total = total + d_ref[t]
        o_ref[t] = total


def vmem():
    return pl.BlockSpec(memory_space=pltpu.VMEM)


def smem():
    return pl.BlockSpec(memory_space=pltpu.SMEM)


def time_features(step, time_weight):
    half = time_weight.shape[0] // 2
    freqs = jnp.exp(-jnp.log(1000.0) * jnp.arange(half, dtype=F32) / half)
    angles = step.astype(F32) * freqs
    feats = jnp.concatenate([jnp.sin(angles), jnp.cos(angles)])
    return jnp.dot(feats, time_weight, precision=lax.Precision.HIGHEST)


def neighbours(value, axis):
    size = lax.axis_size(axis)
    up = [(i, i + 1) for i in range(size - 1)]
    down = [(j, i) for i, j in up]
    return (lambda v: lax.ppermute(v, axis, up)), (lambda v: lax.ppermute(v, axis, down))


def on_device(state, step_index, sched_index, coef_table, time_weight, w_in, w_mid1, w_mid2, w_out):
    own = state[0]
    channels, nz, ny, nx = own.shape
    hid = w_mid1.shape[3]
    slots = lax.axis_size("ta")

    x = jnp.transpose(own.astype(BF16), (2, 1, 0, 3))
    up, down = neighbours(x, "gz")
    x = jnp.concatenate([up(x), x, down(x)], axis=1)
    up, down = neighbours(x, "gy")
    x = jnp.concatenate([up(x[ny - DEPTH :]), x, down(x[:DEPTH])], axis=0)
    x = x.reshape(ny + 2 * DEPTH, (nz + 2 * DEPTH) * channels, nx)

    bias = jnp.broadcast_to(time_features(step_index[0], time_weight)[:, None], (hid, nx))
    ordered = (0, 1, 2, 3, 4, 5)
    w1 = banded(w_in, ordered).reshape(2 * hid, -1)
    w2 = banded(w_mid1, ordered).reshape(2 * hid, -1)
    w3 = banded(w_mid2, ordered).reshape(2 * hid, -1)
    w4 = banded(w_out, (2, 3, 0, 1, 4, 5)).reshape(9 * 2 * channels, -1)
    first = (lax.axis_index("ta") == 0).astype(F32)
    row = lax.dynamic_slice_in_dim(coef_table, sched_index[0], 1, 0)[0]
    coef = jnp.stack([row[0], row[1], first])
    place = jnp.stack(
        [
            lax.axis_index("gz") * nz,
            lax.axis_index("gy") * ny,
            jnp.int32(nz * lax.axis_size("gz")),
            jnp.int32(ny * lax.axis_size("gy")),
        ]
    ).astype(jnp.int32)

    drift = pl.pallas_call(
        net_kernel,
        out_shape=jax.ShapeDtypeStruct(own.shape, F32),
        in_specs=[smem(), smem()] + [vmem()] * 7,
        out_specs=vmem(),
        scratch_shapes=[
            pltpu.VMEM((3,) + x.shape, BF16),
            pltpu.VMEM((3, ny + 6, (nz + 6) * hid, nx), BF16),
            pltpu.VMEM((3, ny + 4, (nz + 4) * hid, nx), BF16),
            pltpu.VMEM((ny + 2, (nz + 2) * hid, nx), BF16),
        ],
        name="net",
    )(place, coef, x, own, bias, w1, w2, w3, w4)

    pieces = drift.reshape(slots, -1, nx)
    pieces = lax.all_to_all(pieces, "ta", 0, 0, tiled=True)
    sums = pl.pallas_call(
        scan_kernel,
        out_shape=jax.ShapeDtypeStruct(pieces.shape, F32),
        in_specs=[vmem()],
        out_specs=vmem(),
        name="scan",
    )(pieces)
    total = lax.all_to_all(sums, "ta", 0, 0, tiled=True)
    return total.reshape(own.shape)[None]


def solution(mesh):
    placed = (P("ta", None, "gz", "gy", None), P("ta"), P("ta"), P(), P(), P(), P(), P(), P())
    return jax.shard_map(
        on_device,
        mesh=mesh,
        in_specs=placed,
        out_specs=P("ta", None, "gz", "gy", None),
        check_vma=False,
    )
```

```python
import functools

import jax
import jax.numpy as jnp
from jax import lax
from jax.experimental import pallas as pl
from jax.experimental.pallas import tpu as pltpu
from jax.sharding import PartitionSpec as P

F32 = jnp.float32
BF16 = jnp.bfloat16
DEPTH = 4


def prep_kernel(sched, coef_ref, feats_ref, tw_ref, wi_ref, wa_ref, wb_ref, wo_ref, coef_o, bias_o, w1, w2, w3, w4):
    def band(w_ref, k):
        taps = [w_ref[dz, k // 3, k % 3] for dz in range(3)]
        none = jnp.zeros_like(taps[0])
        first = jnp.concatenate(taps + [none], axis=0)
        second = jnp.concatenate([none] + taps, axis=0)
        return jnp.concatenate([first, second], axis=1)

    for k in range(9):
        for w_ref, dst in ((wi_ref, w1), (wa_ref, w2), (wb_ref, w3)):
            t = band(w_ref, k).T
            dst[:, k * t.shape[1] : (k + 1) * t.shape[1]] = t
        taps = [wo_ref[dz, k // 3, k % 3] for dz in range(3)]
        none = jnp.zeros_like(taps[0])
        both = [jnp.concatenate(taps + [none], axis=1), jnp.concatenate([none] + taps, axis=1)]
        t = jnp.concatenate(both, axis=0)
        w4[k * t.shape[0] : (k + 1) * t.shape[0], :] = t

    hid = tw_ref.shape[0]
    diag = lax.broadcasted_iota(jnp.int32, (hid, hid), 0) == lax.broadcasted_iota(jnp.int32, (hid, hid), 1)

    def column(row):
        return jnp.sum(jnp.where(diag, row, 0.0), axis=1, keepdims=True)

    bias = jnp.sum(tw_ref[...] * column(feats_ref[...]), axis=0, keepdims=True)
    bias_o[...] = jnp.broadcast_to(column(bias), bias_o.shape)
    picked = lax.broadcasted_iota(jnp.int32, coef_ref.shape, 1) == sched[0]
    both = jnp.sum(jnp.where(picked, coef_ref[...], 0.0), axis=1, keepdims=True)
    for i in range(2):
        coef_o[i] = jnp.broadcast_to(both[i : i + 1], coef_o.shape[1:])


def silu(x):
    return x / (1.0 + jnp.exp(-x))


def shifted(h):
    zero = jnp.zeros((h.shape[0], 1), h.dtype)
    left = jnp.concatenate([zero, h[:, :-1]], axis=1)
    right = jnp.concatenate([h[:, 1:], zero], axis=1)
    return left, h, right


def net_kernel(coef, x_ref, zb_ref, za_ref, yb_ref, ya_ref, own_ref, bias_ref, w1_ref, w2_ref, w3_ref, w4_ref, out_ref, xs, h1, h2, h3):
    channels, nz, ny, nx = own_ref.shape
    hid = bias_ref.shape[0]
    z0, y0 = lax.axis_index("gz") * nz, lax.axis_index("gy") * ny
    z_size, y_size = nz * lax.axis_size("gz"), ny * lax.axis_size("gy")

    rows = nz * channels

    def spread(v, y, start):
        for d, v in enumerate(shifted(v)):
            xs[d, y, start : start + v.shape[0], :] = v

    for y in range(DEPTH):
        spread(yb_ref[y], y, 0)
        spread(ya_ref[y], ny + DEPTH + y, 0)
    for y in range(ny):
        for i, part in enumerate((zb_ref, x_ref, za_ref)):
            spread(part[y], DEPTH + y, i * rows)

    def layer(src, w_ref, dst, depth, unit, dxs):
        off = DEPTH - depth
        pairs_z = (nz + 2 * off) // 2
        n_y = ny + 2 * off
        window = 4 * unit

        def step(zp, _):
            base = pl.multiple_of(zp * (2 * unit), 2 * unit)
            for y in range(0, n_y, 2):
                if depth == 1:
                    rhs = jnp.concatenate(
                        [
                            jnp.concatenate(
                                [src[dx, yy + dy, pl.ds(base, window), :] for dy in range(3) for dx in range(3)],
                                axis=0,
                            )
                            for yy in (y, y + 1)
                        ],
                        axis=1,
                    )
                    acc = jnp.dot(w_ref[...], rhs, preferred_element_type=F32)
                    acc = acc + jnp.tile(bias_ref[...], (2, 2))
                else:
                    acc = None
                    for k in range(9):
                        dy, dx = k // 3, k % 3
                        rhs = jnp.concatenate(
                            [src[dx, yy + dy, pl.ds(base, window), :] for yy in (y, y + 1)], axis=1
                        )
                        part = jnp.dot(
                            w_ref[:, k * window : (k + 1) * window], rhs, preferred_element_type=F32
                        )
                        acc = part if acc is None else acc + part
                h = silu(acc)
                for i in range(2):
                    gy = y0 - off + y + i
                    y_ok = jnp.logical_and(gy >= 0, gy < y_size)
                    for j in range(2):
                        gz = z0 - off + 2 * zp + j
                        ok = jnp.logical_and(y_ok, jnp.logical_and(gz >= 0, gz < z_size))
                        part = h[j * hid : (j + 1) * hid, i * nx : (i + 1) * nx]
                        part = jnp.where(ok, part, 0.0).astype(BF16)
                        rows = pl.ds(pl.multiple_of((2 * zp + j) * hid, hid), hid)
                        if dxs:
                            for d, v in enumerate(shifted(part)):
                                dst[d, y + i, rows, :] = v
                        else:
                            dst[y + i, rows, :] = part
            return 0

        lax.fori_loop(0, pairs_z, step, 0)

    layer(xs, w1_ref, h1, 1, channels, True)
    layer(h1, w2_ref, h2, 2, hid, True)
    layer(h2, w3_ref, h3, 3, hid, False)

    rows = 2 * channels
    lane = lax.broadcasted_iota(jnp.int32, (rows, nx), 1)
    a, b = coef[0], coef[1]
    first = jnp.where(lax.axis_index("ta") == 0, 1.0, 0.0)
    for zp in range(nz // 2):
        parts = []
        for y in range(0, ny + 2, 2):
            rhs = jnp.concatenate(
                [h3[yy, pl.ds(2 * zp * hid, 4 * hid), :] for yy in (y, y + 1)], axis=1
            )
            p = jnp.dot(w4_ref[...], rhs, preferred_element_type=F32)
            parts += [p[:, :nx], p[:, nx:]]
        nets = []
        for y in range(ny):
            t = [
                sum(parts[y + dy][(3 * dy + dx) * rows : (3 * dy + dx + 1) * rows] for dy in range(3))
                for dx in range(3)
            ]
            left = jnp.where(lane == 0, 0.0, pltpu.roll(t[0], 1, 1))
            right = jnp.where(lane == nx - 1, 0.0, pltpu.roll(t[2], nx - 1, 1))
            nets.append(left + t[1] + right)
        for j in range(2):
            net = jnp.stack([n[j * channels : (j + 1) * channels] for n in nets])
            net = jnp.transpose(net, (1, 0, 2))
            own = own_ref[:, 2 * zp + j]
            out_ref[:, 2 * zp + j] = b * net - a * own + first * own


def scan_kernel(d_ref, o_ref):
    total = d_ref[0]
    o_ref[0] = total
    for t in range(1, d_ref.shape[0]):
        total = total + d_ref[t]
        o_ref[t] = total


def add_kernel(d_ref, *refs):
    *more, o_ref = refs
    extra = more[0][...]
    for ref in more[1:]:
        extra = extra + ref[...]
    for t in range(d_ref.shape[0]):
        o_ref[t] = d_ref[t] + extra


def entering(part, axis, team):
    size = lax.axis_size(axis)
    shape, nx = part.shape, part.shape[-1]
    teams = [[first + i for i in range(team)] for first in range(0, size, team)]

    def to(start, end):
        return [(i, j) for i, j in zip(teams[start], teams[end])]

    def swap(v):
        return lax.all_to_all(v, axis, 0, 0, axis_index_groups=teams, tiled=True)

    def local(kernel, shape, *values):
        return pl.pallas_call(
            kernel,
            out_shape=pltpu.VMEM(shape, F32),
            in_specs=[vmem()] * len(values),
            out_specs=vmem(),
        )(*held(*values))

    pieces = swap(part.reshape(team, -1, nx))
    sums = local(scan_kernel, pieces.shape, pieces)
    total = sums[team - 1]
    first = lax.ppermute(total, axis, to(0, 1))
    third = lax.ppermute(total, axis, to(2, 3))
    half = total + first
    near = lax.ppermute(half, axis, to(1, 2))
    far = lax.ppermute(half, axis, to(1, 3))
    return swap(local(add_kernel, sums.shape, sums, first, third, near, far)).reshape(shape)


def vmem():
    return pl.BlockSpec(memory_space=pltpu.VMEM)


def held(*values):
    return [pltpu.with_memory_space_constraint(v, pltpu.VMEM) for v in values]


def net_call(coef, x, zb, za, yb, ya, own, bias, w1, w2, w3, w4):
    channels, nz, ny, nx = own.shape
    hid = bias.shape[0]
    return pl.pallas_call(
        net_kernel,
        out_shape=pltpu.VMEM(own.shape, F32),
        in_specs=[vmem()] * 12,
        out_specs=vmem(),
        scratch_shapes=[
            pltpu.VMEM((3, ny + 2 * DEPTH, (nz + 2 * DEPTH) * channels, nx), BF16),
            pltpu.VMEM((3, ny + 6, (nz + 6) * hid, nx), BF16),
            pltpu.VMEM((3, ny + 4, (nz + 4) * hid, nx), BF16),
            pltpu.VMEM((ny + 2, (nz + 2) * hid, nx), BF16),
        ],
        name="net",
    )(*held(coef, x, zb, za, yb, ya), own, *held(bias, w1, w2, w3, w4))


def features(step, half):
    freqs = jnp.exp(-jnp.log(1000.0) * jnp.arange(half, dtype=F32) / half)
    angles = step.astype(F32) * freqs
    return jnp.concatenate([jnp.sin(angles), jnp.cos(angles)])


def exchange(up, down, axis):
    ahead = [(i, i + 1) for i in range(lax.axis_size(axis) - 1)]
    return lax.ppermute(up, axis, ahead), lax.ppermute(down, axis, [(j, i) for i, j in ahead])


def on_device(state, step_index, sched_index, coef_table, time_weight, w_in, w_mid1, w_mid2, w_out):
    own = state[0]
    channels, nz, ny, nx = own.shape
    hid = w_mid1.shape[3]

    x = jnp.transpose(own.astype(BF16), (2, 1, 0, 3)).reshape(ny, nz * channels, nx)
    zb, za = exchange(x, x, "gz")
    tall = [jnp.concatenate([v[part] for v in (zb, x, za)], axis=1) for part in (slice(ny - DEPTH, ny), slice(0, DEPTH))]
    yb, ya = exchange(tall[0], tall[1], "gy")

    feats = features(step_index[0], hid // 2)[None]
    inputs = (feats, time_weight, w_in, w_mid1, w_mid2, jnp.swapaxes(w_out, 3, 4))
    outputs = [
        pltpu.VMEM(shape, dtype)
        for shape, dtype in (
            ((2, channels, nx), F32),
            ((hid, nx), F32),
            ((2 * hid, 36 * channels), BF16),
            ((2 * hid, 36 * hid), BF16),
            ((2 * hid, 36 * hid), BF16),
            ((18 * channels, 4 * hid), BF16),
        )
    ]
    coef, bias, w1, w2, w3, w4 = pl.pallas_call(
        prep_kernel,
        out_shape=outputs,
        in_specs=[pl.BlockSpec(memory_space=pltpu.SMEM)] + [vmem()] * (1 + len(inputs)),
        out_specs=[vmem()] * len(outputs),
        name="prep",
    )(sched_index, coef_table.T, *inputs)

    drift = net_call(coef, x, zb, za, yb, ya, own, bias, w1, w2, w3, w4)

    return entering(drift, "ta", 4)[None]


def solution(mesh):
    placed = (P("ta", None, "gz", "gy", None), P("ta"), P("ta"), P(), P(), P(), P(), P(), P())
    return jax.shard_map(
        on_device,
        mesh=mesh,
        in_specs=placed,
        out_specs=P("ta", None, "gz", "gy", None),
        check_vma=False,
    )
```

```python
import functools

import jax
import jax.numpy as jnp
from jax import lax
from jax.experimental import pallas as pl
from jax.experimental.pallas import tpu as pltpu
from jax.sharding import PartitionSpec as P

F32 = jnp.float32
BF16 = jnp.bfloat16
DEPTH = 4


def prep_kernel(sched, coef_ref, feats_ref, tw_ref, wi_ref, wa_ref, wb_ref, wo_ref, coef_o, bias_o, w1, w2, w3, w4):
    def band(w_ref, k):
        taps = [w_ref[dz, k // 3, k % 3] for dz in range(3)]
        none = jnp.zeros_like(taps[0])
        first = jnp.concatenate(taps + [none], axis=0)
        second = jnp.concatenate([none] + taps, axis=0)
        return jnp.concatenate([first, second], axis=1)

    def flipped(v):
        n = v.shape[1]
        unit = (
            lax.broadcasted_iota(jnp.int32, (n, n), 0) == lax.broadcasted_iota(jnp.int32, (n, n), 1)
        ).astype(BF16)
        return lax.dot_general(unit, v, (((1,), (1,)), ((), ())), preferred_element_type=F32).astype(BF16)

    for k in range(9):
        for w_ref, dst in ((wi_ref, w1), (wa_ref, w2), (wb_ref, w3)):
            t = flipped(band(w_ref, k))
            dst[:, k * t.shape[1] : (k + 1) * t.shape[1]] = t
        taps = [wo_ref[dz, k // 3, k % 3] for dz in range(3)]
        none = jnp.zeros_like(taps[0])
        both = [jnp.concatenate(taps + [none], axis=1), jnp.concatenate([none] + taps, axis=1)]
        t = jnp.concatenate(both, axis=0)
        w4[k * t.shape[0] : (k + 1) * t.shape[0], :] = t

    hid = tw_ref.shape[0]
    diag = lax.broadcasted_iota(jnp.int32, (hid, hid), 0) == lax.broadcasted_iota(jnp.int32, (hid, hid), 1)

    def column(row):
        return jnp.sum(jnp.where(diag, row, 0.0), axis=1, keepdims=True)

    bias = jnp.sum(tw_ref[...] * column(feats_ref[...]), axis=0, keepdims=True)
    bias_o[...] = jnp.broadcast_to(column(bias), bias_o.shape)
    picked = lax.broadcasted_iota(jnp.int32, coef_ref.shape, 1) == sched[0]
    both = jnp.sum(jnp.where(picked, coef_ref[...], 0.0), axis=1, keepdims=True)
    for i in range(2):
        coef_o[i] = jnp.broadcast_to(both[i : i + 1], coef_o.shape[1:])


def silu(x):
    return x / (1.0 + jnp.exp(-x))


def shifted(h):
    zero = jnp.zeros((h.shape[0], 1), h.dtype)
    left = jnp.concatenate([zero, h[:, :-1]], axis=1)
    right = jnp.concatenate([h[:, 1:], zero], axis=1)
    return left, h, right


def net_kernel(coef, x_ref, zb_ref, za_ref, yb_ref, ya_ref, own_ref, bias_ref, w1_ref, w2_ref, w3_ref, w4_ref, out_ref, xs, h1, h2, h3):
    channels, nz, ny, nx = own_ref.shape
    hid = bias_ref.shape[0]
    z0, y0 = lax.axis_index("gz") * nz, lax.axis_index("gy") * ny
    z_size, y_size = nz * lax.axis_size("gz"), ny * lax.axis_size("gy")

    rows = nz * channels

    def spread(v, y, start):
        for d, v in enumerate(shifted(v)):
            xs[d, y, start : start + v.shape[0], :] = v

    def ordered(odd, first, second):
        first, second = first.astype(F32), second.astype(F32)
        return jnp.where(odd, first, second).astype(BF16), jnp.where(odd, second, first).astype(BF16)

    odd_y, odd_z = is_odd("gy"), is_odd("gz")
    for y in range(DEPTH):
        before, after = ordered(odd_y, yb_ref[y], ya_ref[y])
        spread(before, y, 0)
        spread(after, ny + DEPTH + y, 0)
    for y in range(ny):
        before, after = ordered(odd_z, zb_ref[y], za_ref[y])
        for i, part in enumerate((before, x_ref[y], after)):
            spread(part, DEPTH + y, i * rows)

    def layer(src, w_ref, dst, depth, unit, dxs):
        off = DEPTH - depth
        pairs_z = (nz + 2 * off) // 2
        n_y = ny + 2 * off
        window = 4 * unit

        def step(zp, _):
            base = pl.multiple_of(zp * (2 * unit), 2 * unit)
            for y in range(0, n_y, 2):
                if depth == 1:
                    rhs = jnp.concatenate(
                        [
                            jnp.concatenate(
                                [src[dx, yy + dy, pl.ds(base, window), :] for dy in range(3) for dx in range(3)],
                                axis=0,
                            )
                            for yy in (y, y + 1)
                        ],
                        axis=1,
                    )
                    acc = jnp.dot(w_ref[...], rhs, preferred_element_type=F32)
                    acc = acc + jnp.tile(bias_ref[...], (2, 2))
                else:
                    acc = None
                    for k in range(9):
                        dy, dx = k // 3, k % 3
                        rhs = jnp.concatenate(
                            [src[dx, yy + dy, pl.ds(base, window), :] for yy in (y, y + 1)], axis=1
                        )
                        part = jnp.dot(
                            w_ref[:, k * window : (k + 1) * window], rhs, preferred_element_type=F32
                        )
                        acc = part if acc is None else acc + part
                h = silu(acc)
                for i in range(2):
                    gy = y0 - off + y + i
                    y_ok = jnp.logical_and(gy >= 0, gy < y_size)
                    for j in range(2):
                        gz = z0 - off + 2 * zp + j
                        ok = jnp.logical_and(y_ok, jnp.logical_and(gz >= 0, gz < z_size))
                        part = h[j * hid : (j + 1) * hid, i * nx : (i + 1) * nx]
                        part = jnp.where(ok, part, 0.0).astype(BF16)
                        rows = pl.ds(pl.multiple_of((2 * zp + j) * hid, hid), hid)
                        if dxs:
                            for d, v in enumerate(shifted(part)):
                                dst[d, y + i, rows, :] = v
                        else:
                            dst[y + i, rows, :] = part
            return 0

        lax.fori_loop(0, pairs_z, step, 0, unroll=True)

    layer(xs, w1_ref, h1, 1, channels, True)
    layer(h1, w2_ref, h2, 2, hid, True)
    layer(h2, w3_ref, h3, 3, hid, False)

    rows = 2 * channels
    lane = lax.broadcasted_iota(jnp.int32, (rows, nx), 1)
    a, b = coef[0], coef[1]
    first = jnp.where(lax.axis_index("ta") == 0, 1.0, 0.0)
    for zp in range(nz // 2):
        parts = []
        for y in range(0, ny + 2, 2):
            rhs = jnp.concatenate(
                [h3[yy, pl.ds(2 * zp * hid, 4 * hid), :] for yy in (y, y + 1)], axis=1
            )
            p = jnp.dot(w4_ref[...], rhs, preferred_element_type=F32)
            parts += [p[:, :nx], p[:, nx:]]
        nets = []
        for y in range(ny):
            t = [
                sum(parts[y + dy][(3 * dy + dx) * rows : (3 * dy + dx + 1) * rows] for dy in range(3))
                for dx in range(3)
            ]
            left = jnp.where(lane == 0, 0.0, pltpu.roll(t[0], 1, 1))
            right = jnp.where(lane == nx - 1, 0.0, pltpu.roll(t[2], nx - 1, 1))
            nets.append(left + t[1] + right)
        for j in range(2):
            net = jnp.stack([n[j * channels : (j + 1) * channels] for n in nets])
            net = jnp.transpose(net, (1, 0, 2))
            own = own_ref[:, 2 * zp + j]
            out_ref[:, 2 * zp + j] = b * net - a * own + first * own


def scan_kernel(d_ref, o_ref):
    total = d_ref[0]
    o_ref[0] = total
    for t in range(1, d_ref.shape[0]):
        total = total + d_ref[t]
        o_ref[t] = total


def add_kernel(d_ref, *refs):
    *more, o_ref = refs
    extra = more[0][...]
    for ref in more[1:]:
        extra = extra + ref[...]
    for t in range(d_ref.shape[0]):
        o_ref[t] = d_ref[t] + extra


def entering(part, axis, team):
    size = lax.axis_size(axis)
    shape, nx = part.shape, part.shape[-1]
    teams = [[first + i for i in range(team)] for first in range(0, size, team)]

    def to(start, end):
        return [(i, j) for i, j in zip(teams[start], teams[end])]

    def swap(v):
        return lax.all_to_all(v, axis, 0, 0, axis_index_groups=teams, tiled=True)

    def local(kernel, shape, *values):
        return pl.pallas_call(
            kernel,
            out_shape=pltpu.VMEM(shape, F32),
            in_specs=[vmem()] * len(values),
            out_specs=vmem(),
        )(*held(*values))

    pieces = swap(part.reshape(team, -1, nx))
    sums = local(scan_kernel, pieces.shape, pieces)
    total = sums[team - 1]
    first = lax.ppermute(total, axis, to(0, 1))
    half = total + first
    far = lax.ppermute(half, axis, to(1, 3))
    near = lax.ppermute(half, axis, to(1, 2) + to(2, 3))
    return swap(local(add_kernel, sums.shape, sums, first, near, far)).reshape(shape)


def vmem():
    return pl.BlockSpec(memory_space=pltpu.VMEM)


def held(*values):
    return [pltpu.with_memory_space_constraint(v, pltpu.VMEM) for v in values]


def net_call(coef, x, zb, za, yb, ya, own, bias, w1, w2, w3, w4):
    channels, nz, ny, nx = own.shape
    hid = bias.shape[0]
    return pl.pallas_call(
        net_kernel,
        out_shape=pltpu.VMEM(own.shape, F32),
        in_specs=[vmem()] * 12,
        out_specs=vmem(),
        scratch_shapes=[
            pltpu.VMEM((3, ny + 2 * DEPTH, (nz + 2 * DEPTH) * channels, nx), BF16),
            pltpu.VMEM((3, ny + 6, (nz + 6) * hid, nx), BF16),
            pltpu.VMEM((3, ny + 4, (nz + 4) * hid, nx), BF16),
            pltpu.VMEM((ny + 2, (nz + 2) * hid, nx), BF16),
        ],
        compiler_params=pltpu.CompilerParams(vmem_limit_bytes=24 << 20),
        name="net",
    )(*held(coef, x, zb, za, yb, ya), own, *held(bias, w1, w2, w3, w4))


def features(step, half):
    freqs = jnp.exp(-jnp.log(1000.0) * jnp.arange(half, dtype=F32) / half)
    angles = step.astype(F32) * freqs
    return jnp.concatenate([jnp.sin(angles), jnp.cos(angles)])


def is_odd(axis):
    return lax.rem(lax.axis_index(axis), 2) == 1


def exchange(up, down, axis):
    size = lax.axis_size(axis)
    got = []
    for start in (0, 1):
        pairs = [(i, i + 1) for i in range(start, size - 1, 2)]
        send = up if up is down else jnp.where(is_odd(axis) == (start == 1), up, down)
        got.append(lax.ppermute(send, axis, pairs + [(j, i) for i, j in pairs]))
    return got


def on_device(state, step_index, sched_index, coef_table, time_weight, w_in, w_mid1, w_mid2, w_out):
    own = state[0]
    channels, nz, ny, nx = own.shape
    hid = w_mid1.shape[3]

    x = jnp.transpose(own.astype(BF16), (2, 1, 0, 3)).reshape(ny, nz * channels, nx)
    zb, za = exchange(x, x, "gz")
    odd = is_odd("gz")
    column = (jnp.where(odd, zb, za), x, jnp.where(odd, za, zb))
    tall = [jnp.concatenate([v[part] for v in column], axis=1) for part in (slice(ny - DEPTH, ny), slice(0, DEPTH))]
    yb, ya = exchange(tall[0], tall[1], "gy")

    feats = features(step_index[0], hid // 2)[None]
    inputs = (feats, time_weight, w_in, w_mid1, w_mid2, jnp.swapaxes(w_out, 3, 4))
    outputs = [
        pltpu.VMEM(shape, dtype)
        for shape, dtype in (
            ((2, channels, nx), F32),
            ((hid, nx), F32),
            ((2 * hid, 36 * channels), BF16),
            ((2 * hid, 36 * hid), BF16),
            ((2 * hid, 36 * hid), BF16),
            ((18 * channels, 4 * hid), BF16),
        )
    ]
    coef, bias, w1, w2, w3, w4 = pl.pallas_call(
        prep_kernel,
        out_shape=outputs,
        in_specs=[pl.BlockSpec(memory_space=pltpu.SMEM)] + [vmem()] * (1 + len(inputs)),
        out_specs=[vmem()] * len(outputs),
        compiler_params=pltpu.CompilerParams(vmem_limit_bytes=8 << 20),
        name="prep",
    )(sched_index, *held(coef_table.T, *inputs))

    drift = net_call(coef, x, zb, za, yb, ya, own, bias, w1, w2, w3, w4)

    return entering(drift, "ta", 4)[None]


def solution(mesh):
    placed = (P("ta", None, "gz", "gy", None), P("ta"), P("ta"), P(), P(), P(), P(), P(), P())
    return jax.shard_map(
        on_device,
        mesh=mesh,
        in_specs=placed,
        out_specs=P("ta", None, "gz", "gy", None),
        check_vma=False,
    )
```

```python
import jax
import jax.numpy as jnp
from jax import lax
from jax.experimental import pallas as pl
from jax.experimental.pallas import tpu as pltpu
from jax.sharding import PartitionSpec as P


F32 = jnp.float32
BF16 = jnp.bfloat16
DEPTH = 4


def prep_kernel(sched, coef_ref, feats_ref, tw_ref, wi_ref, wa_ref, wb_ref, wo_ref, coef_o, bias_o, w1, w2, w3, w4):
    def band(w_ref, k):
        taps = [w_ref[dz, k // 3, k % 3] for dz in range(3)]
        none = jnp.zeros_like(taps[0])
        first = jnp.concatenate(taps + [none], axis=0)
        second = jnp.concatenate([none] + taps, axis=0)
        return jnp.concatenate([first, second], axis=1)

    def flipped(v):
        n = v.shape[1]
        unit = (
            lax.broadcasted_iota(jnp.int32, (n, n), 0) == lax.broadcasted_iota(jnp.int32, (n, n), 1)
        ).astype(BF16)
        return lax.dot_general(unit, v, (((1,), (1,)), ((), ())), preferred_element_type=F32).astype(BF16)

    for k in range(9):
        for w_ref, dst in ((wi_ref, w1), (wa_ref, w2), (wb_ref, w3)):
            t = flipped(band(w_ref, k))
            dst[:, k * t.shape[1] : (k + 1) * t.shape[1]] = t
        taps = [wo_ref[dz, k // 3, k % 3] for dz in range(3)]
        none = jnp.zeros_like(taps[0])
        both = [jnp.concatenate(taps + [none], axis=1), jnp.concatenate([none] + taps, axis=1)]
        t = jnp.concatenate(both, axis=0)
        w4[k * t.shape[0] : (k + 1) * t.shape[0], :] = t

    hid = tw_ref.shape[0]
    diag = lax.broadcasted_iota(jnp.int32, (hid, hid), 0) == lax.broadcasted_iota(jnp.int32, (hid, hid), 1)

    def column(row):
        return jnp.sum(jnp.where(diag, row, 0.0), axis=1, keepdims=True)

    bias = jnp.sum(tw_ref[...] * column(feats_ref[...]), axis=0, keepdims=True)
    bias_o[...] = jnp.broadcast_to(column(bias), bias_o.shape)
    picked = lax.broadcasted_iota(jnp.int32, coef_ref.shape, 1) == sched[0]
    both = jnp.sum(jnp.where(picked, coef_ref[...], 0.0), axis=1, keepdims=True)
    for i in range(2):
        coef_o[i] = jnp.broadcast_to(both[i : i + 1], coef_o.shape[1:])


def silu(x):
    half = 0.5 * x
    return half + half * jnp.tanh(half)


def shifted(h):
    zero = jnp.zeros((h.shape[0], 1), h.dtype)
    left = jnp.concatenate([zero, h[:, :-1]], axis=1)
    right = jnp.concatenate([h[:, 1:], zero], axis=1)
    return left, h, right


def net_kernel(coef, x_ref, zb_ref, za_ref, yb_ref, ya_ref, own_ref, bias_ref, w1_ref, w2_ref, w3_ref, w4_ref, out_ref, xs, h1, h2, h3):
    channels, nz, ny, nx = own_ref.shape
    hid = bias_ref.shape[0]
    z0, y0 = lax.axis_index("gz") * nz, lax.axis_index("gy") * ny
    z_size, y_size = nz * lax.axis_size("gz"), ny * lax.axis_size("gy")

    rows = nz * channels

    def spread(v, y, start):
        for d, v in enumerate(shifted(v)):
            xs[d, y, start : start + v.shape[0], :] = v

    def ordered(odd, first, second):
        first, second = first.astype(F32), second.astype(F32)
        return jnp.where(odd, first, second).astype(BF16), jnp.where(odd, second, first).astype(BF16)

    odd_y, odd_z = is_odd("gy"), is_odd("gz")
    for y in range(DEPTH):
        before, after = ordered(odd_y, yb_ref[y], ya_ref[y])
        spread(before, y, 0)
        spread(after, ny + DEPTH + y, 0)
    for y in range(ny):
        before, after = ordered(odd_z, zb_ref[y], za_ref[y])
        for i, part in enumerate((before, x_ref[y], after)):
            spread(part, DEPTH + y, i * rows)

    def layer(src, w_ref, dst, depth, unit, dxs):
        off = DEPTH - depth
        pairs_z = (nz + 2 * off) // 2
        n_y = ny + 2 * off
        window = 4 * unit

        def step(zp, _):
            base = pl.multiple_of(zp * (2 * unit), 2 * unit)
            for y in range(0, n_y, 2):
                if depth == 1:
                    rhs = jnp.concatenate(
                        [
                            jnp.concatenate(
                                [src[dx, yy + dy, pl.ds(base, window), :] for dy in range(3) for dx in range(3)],
                                axis=0,
                            )
                            for yy in (y, y + 1)
                        ],
                        axis=1,
                    )
                    acc = jnp.dot(w_ref[...], rhs, preferred_element_type=F32)
                    acc = acc + jnp.tile(bias_ref[...], (2, 2))
                else:
                    acc = None
                    for k in range(9):
                        dy, dx = k // 3, k % 3
                        rhs = jnp.concatenate(
                            [src[dx, yy + dy, pl.ds(base, window), :] for yy in (y, y + 1)], axis=1
                        )
                        part = jnp.dot(
                            w_ref[:, k * window : (k + 1) * window], rhs, preferred_element_type=F32
                        )
                        acc = part if acc is None else acc + part
                h = silu(acc)
                for i in range(2):
                    gy = y0 - off + y + i
                    y_ok = jnp.logical_and(gy >= 0, gy < y_size)
                    for j in range(2):
                        gz = z0 - off + 2 * zp + j
                        ok = jnp.logical_and(y_ok, jnp.logical_and(gz >= 0, gz < z_size))
                        part = h[j * hid : (j + 1) * hid, i * nx : (i + 1) * nx]
                        part = jnp.where(ok, part, 0.0).astype(BF16)
                        rows = pl.ds(pl.multiple_of((2 * zp + j) * hid, hid), hid)
                        if dxs:
                            for d, v in enumerate(shifted(part)):
                                dst[d, y + i, rows, :] = v
                        else:
                            dst[y + i, rows, :] = part
            return 0

        lax.fori_loop(0, pairs_z, step, 0, unroll=True)

    layer(xs, w1_ref, h1, 1, channels, True)
    layer(h1, w2_ref, h2, 2, hid, True)
    layer(h2, w3_ref, h3, 3, hid, False)

    rows = 2 * channels
    lane = lax.broadcasted_iota(jnp.int32, (rows, nx), 1)
    a, b = coef[0], coef[1]
    first = jnp.where(lax.axis_index("ta") == 0, 1.0, 0.0)
    for zp in range(nz // 2):
        parts = []
        for y in range(0, ny + 2, 2):
            rhs = jnp.concatenate(
                [h3[yy, pl.ds(2 * zp * hid, 4 * hid), :] for yy in (y, y + 1)], axis=1
            )
            p = jnp.dot(w4_ref[...], rhs, preferred_element_type=F32)
            parts += [p[:, :nx], p[:, nx:]]
        nets = []
        for y in range(ny):
            t = [
                sum(parts[y + dy][(3 * dy + dx) * rows : (3 * dy + dx + 1) * rows] for dy in range(3))
                for dx in range(3)
            ]
            left = jnp.where(lane == 0, 0.0, pltpu.roll(t[0], 1, 1))
            right = jnp.where(lane == nx - 1, 0.0, pltpu.roll(t[2], nx - 1, 1))
            nets.append(left + t[1] + right)
        for j in range(2):
            net = jnp.stack([n[j * channels : (j + 1) * channels] for n in nets])
            net = jnp.transpose(net, (1, 0, 2))
            own = own_ref[:, 2 * zp + j]
            out_ref[:, 2 * zp + j] = b * net - a * own + first * own


def scan_kernel(d_ref, o_ref):
    total = d_ref[0]
    o_ref[0] = total
    for t in range(1, d_ref.shape[0]):
        total = total + d_ref[t]
        o_ref[t] = total


def add_kernel(d_ref, *refs):
    *more, o_ref = refs
    extra = more[0][...]
    for ref in more[1:]:
        extra = extra + ref[...]
    for t in range(d_ref.shape[0]):
        o_ref[t] = d_ref[t] + extra


def entering(part, axis, team):
    size = lax.axis_size(axis)
    shape, nx = part.shape, part.shape[-1]
    teams = [[first + i for i in range(team)] for first in range(0, size, team)]

    def to(start, end):
        return [(i, j) for i, j in zip(teams[start], teams[end])]

    def swap(v):
        return lax.all_to_all(v, axis, 0, 0, axis_index_groups=teams, tiled=True)

    def local(kernel, shape, *values):
        return pl.pallas_call(
            kernel,
            out_shape=pltpu.VMEM(shape, F32),
            in_specs=[vmem()] * len(values),
            out_specs=vmem(),
        )(*held(*values))

    pieces = swap(part.reshape(team, -1, nx))
    sums = local(scan_kernel, pieces.shape, pieces)
    total = sums[team - 1]
    first = lax.ppermute(total, axis, to(0, 1))
    wrap = lax.ppermute(total, axis, to(0, 3))
    far = lax.ppermute(total, axis, to(1, 3))
    half = total + first
    near = lax.ppermute(half, axis, to(1, 2) + to(2, 3))
    return swap(local(add_kernel, sums.shape, sums, first, wrap, far, near)).reshape(shape)


def vmem():
    return pl.BlockSpec(memory_space=pltpu.VMEM)


def held(*values):
    return [pltpu.with_memory_space_constraint(v, pltpu.VMEM) for v in values]


def net_call(coef, x, zb, za, yb, ya, own, bias, w1, w2, w3, w4):
    channels, nz, ny, nx = own.shape
    hid = bias.shape[0]
    return pl.pallas_call(
        net_kernel,
        out_shape=pltpu.VMEM(own.shape, F32),
        in_specs=[vmem()] * 12,
        out_specs=vmem(),
        scratch_shapes=[
            pltpu.VMEM((3, ny + 2 * DEPTH, (nz + 2 * DEPTH) * channels, nx), BF16),
            pltpu.VMEM((3, ny + 6, (nz + 6) * hid, nx), BF16),
            pltpu.VMEM((3, ny + 4, (nz + 4) * hid, nx), BF16),
            pltpu.VMEM((ny + 2, (nz + 2) * hid, nx), BF16),
        ],
        compiler_params=pltpu.CompilerParams(vmem_limit_bytes=24 << 20),
        name="net",
    )(*held(coef, x, zb, za, yb, ya), own, *held(bias, w1, w2, w3, w4))


def features(step, half):
    freqs = jnp.exp(-jnp.log(1000.0) * jnp.arange(half, dtype=F32) / half)
    angles = step.astype(F32) * freqs
    return jnp.concatenate([jnp.sin(angles), jnp.cos(angles)])


def is_odd(axis):
    return lax.rem(lax.axis_index(axis), 2) == 1


def exchange(up, down, axis):
    size = lax.axis_size(axis)
    got = {}
    for start in (1, 0):
        pairs = [(i, i + 1) for i in range(start, size - 1, 2)]
        send = up if up is down else jnp.where(is_odd(axis) == (start == 1), up, down)
        got[start] = lax.ppermute(send, axis, pairs + [(j, i) for i, j in pairs])
    return got[0], got[1]


def on_device(state, step_index, sched_index, coef_table, time_weight, w_in, w_mid1, w_mid2, w_out):
    own = state[0]
    channels, nz, ny, nx = own.shape
    hid = w_mid1.shape[3]

    x = jnp.transpose(own.astype(BF16), (2, 1, 0, 3)).reshape(ny, nz * channels, nx)
    zb, za = exchange(x, x, "gz")
    odd = is_odd("gz")
    column = (jnp.where(odd, zb, za), x, jnp.where(odd, za, zb))
    tall = [jnp.concatenate([v[part] for v in column], axis=1) for part in (slice(ny - DEPTH, ny), slice(0, DEPTH))]
    yb, ya = exchange(tall[0], tall[1], "gy")

    feats = features(step_index[0], hid // 2)[None]
    inputs = (feats, time_weight, w_in, w_mid1, w_mid2, jnp.swapaxes(w_out, 3, 4))
    outputs = [
        pltpu.VMEM(shape, dtype)
        for shape, dtype in (
            ((2, channels, nx), F32),
            ((hid, nx), F32),
            ((2 * hid, 36 * channels), BF16),
            ((2 * hid, 36 * hid), BF16),
            ((2 * hid, 36 * hid), BF16),
            ((18 * channels, 4 * hid), BF16),
        )
    ]
    coef, bias, w1, w2, w3, w4 = pl.pallas_call(
        prep_kernel,
        out_shape=outputs,
        in_specs=[pl.BlockSpec(memory_space=pltpu.SMEM)] + [vmem()] * (1 + len(inputs)),
        out_specs=[vmem()] * len(outputs),
        compiler_params=pltpu.CompilerParams(vmem_limit_bytes=8 << 20),
        name="prep",
    )(sched_index, *held(coef_table.T, *inputs))

    drift = net_call(coef, x, zb, za, yb, ya, own, bias, w1, w2, w3, w4)

    return entering(drift, "ta", 4)[None]


def solution(mesh):
    placed = (P("ta", None, "gz", "gy", None), P("ta"), P("ta"), P(), P(), P(), P(), P(), P())
    return jax.shard_map(
        on_device,
        mesh=mesh,
        in_specs=placed,
        out_specs=P("ta", None, "gz", "gy", None),
        check_vma=False,
    )
```
